512 devices in a mesh: tm: 16 (over z, core), env: 32 (over x, y).
Axes of the slice: x: 4, y: 8, z: 8, core: 2. Of those that a mesh axis runs over, the one named last changes fastest.
Arguments:
- rewards: float32 [4096, 4096], P('tm', 'env'), may hold values from -6 to 6
- dones: int32 [4096, 4096], P('tm', 'env'), may hold values 0 or 1
- horizon: float32 [4096], P('env'), may hold values from 20 to 8192
- bootstrap: float32 [4096], P('env'), may hold values from -96 to 96
- prior_mean: float32 [1], replicated, may hold values from -240 to 240
- prior_var: float32 [1], replicated, may hold values from 100 to 3000
Outputs:
- scaled_rewards: float32 [4096, 4096], P('tm', 'env')
- scaled_returns: float32 [4096, 4096], P('tm', 'env')
- running_stats: float32 [2], replicated
The draws below stay inside these ranges and needn't reach their ends.
All inputs are finite; a program needn't handle non-finite values. No bound on the sum of `dones` on one device may be relied on, other than what follows from the above.
Results may differ from the reference program's by a relative error of at most 0.0003.
Values sent between devices are 32-bit elements; how exact they have to be, the bound alone decides.
No kernel may reach another device: no remote copies, remote signals or barrier semaphores. Data moves between devices by JAX's collectives and lax.ppermute only.
A program may use at most 64 MiB of HBM per device.

```python
import math
import jax
import jax.numpy as jnp
from jax import lax

TIME = 4096
ENVS = 4096
PRIOR = 16777216


def place_ends(result, key, least, largest):
    place = [jax.random.randint(jax.random.fold_in(key, axis), (), 0, length) for axis, length in enumerate(result.shape)]
    widest = result.shape.index(max(result.shape))
    beside = place[:widest] + [(place[widest] + 1) % result.shape[widest]] + place[widest + 1:]
    return result.at[tuple(place)].set(least).at[tuple(beside)].set(largest)


def level_of(rng, shape, pieces, low, largest):
    def one(dim, parts):
        steps = jax.random.uniform(jax.random.fold_in(jax.random.fold_in(rng, 6), dim), (parts,), jnp.float32, low / len(pieces), largest / len(pieces))
        return jnp.repeat(jnp.exp(steps), shape[dim] // parts).reshape((-1,) + (1,) * (len(shape) - dim - 1))

    loudness = one(*pieces[0])
    for cut in pieces[1:]:
        loudness = loudness * one(*cut)
    return loudness


def bell_draw(stream_key, extent, scale, reach, pieces=(), kind=jnp.bfloat16):
    drawn = jax.random.normal(stream_key, extent, jnp.float32) * scale
    if len(pieces) > 0:
        drawn = level_of(stream_key, extent, pieces, -0.22, 0.18) * drawn
    return jnp.clip(drawn, min=-reach, max=reach).astype(kind)


def setup_inputs(seed: int = 0) -> dict:
    arg_keys = jax.random.split(jax.random.key(seed), 7)
    rewards = bell_draw(arg_keys[0], (TIME, ENVS), 1.0, 6.0, ((0, 16), (1, 32)), jnp.float32)
    dones = place_ends((jax.random.randint(arg_keys[1], (TIME, ENVS), 0, 4 * TIME) < 1).astype(jnp.int32), jax.random.fold_in(arg_keys[1], 1), 0, 1)
    horizon = jnp.clip(jnp.exp(math.log(8192.0) - 6.015181 * jax.random.uniform(arg_keys[2], (ENVS,), jnp.float32) ** level_of(arg_keys[2], (ENVS,), ((0, 32),), -0.2, 0.2)), 20.0, 8192.0)
    bootstrap = bell_draw(arg_keys[3], (ENVS,), 16.0, 96.0, ((0, 32),), jnp.float32)
    prior_mean = bell_draw(arg_keys[4], (1,), 40.0, 240.0, (), jnp.float32)
    prior_var = jnp.clip(jnp.exp(jax.random.uniform(arg_keys[5], (1,), jnp.float32, math.log(100.0), math.log(3000.0))), 100.0, 3000.0)
    return {"rewards": rewards, "dones": dones, "horizon": horizon, "bootstrap": bootstrap, "prior_mean": prior_mean, "prior_var": prior_var}


def reference(rewards, dones, horizon, bootstrap, prior_mean, prior_var):
    discount = 1.0 - 1.0 / horizon
    factor = discount[None, :] * (1.0 - dones.astype(jnp.float32))

    def backward(carried, inputs):
        reward_row, factor_row = inputs
        updated = reward_row + factor_row * carried
        return (updated, updated)
    final_carry, returns = lax.scan(backward, bootstrap, (rewards, factor), reverse=True)
    entries = jnp.float32(returns.size)
    average = jnp.sum(returns) / entries
    spread = jnp.sum((returns - average) * (returns - average))
    prior_count = jnp.float32(PRIOR)
    merged = prior_count + entries
    delta = average - prior_mean[0]
    new_mean = prior_mean[0] + delta * entries / merged
    new_spread = prior_var[0] * prior_count + spread + delta * delta * prior_count * entries / merged
    variance = new_spread / merged
    inverse = 1.0 / jnp.sqrt(variance + 1e-08)
    return (rewards * inverse, returns * inverse, jnp.stack([new_mean, variance]))
```

```python
import functools

import jax
import jax.numpy as jnp
from jax import lax
from jax.experimental import pallas as pl
from jax.experimental.pallas import tpu as pltpu
from jax.sharding import PartitionSpec as P

SUB = 8
VMEM = pltpu.VMEM
SMEM = pltpu.SMEM


def in_vmem(array):
    return pltpu.with_memory_space_constraint(array, VMEM)


def exclusive(summed, product):
    row = lax.broadcasted_iota(jnp.int32, summed.shape, 0)
    for shift in (1, 2, 4):
        inside = row < SUB - shift
        later_sum = jnp.where(inside, pltpu.roll(summed, SUB - shift, 0), 0.0)
        later_product = jnp.where(inside, pltpu.roll(product, SUB - shift, 0), 1.0)
        summed = summed + product * later_sum
        product = product * later_product
    inside = row < SUB - 1
    enter_sum = jnp.where(inside, pltpu.roll(summed, SUB - 1, 0), 0.0)
    enter_product = jnp.where(inside, pltpu.roll(product, SUB - 1, 0), 1.0)
    return enter_sum, enter_product, summed[0:1], product[0:1]


def block_kernel(copies, mean_ref, rewards_ref, dones_ref, horizon_ref, sent_ref, enter_ref):
    steps, lanes = rewards_ref.shape[0] // SUB, rewards_ref.shape[1]
    center = mean_ref[0]
    discount = jnp.broadcast_to(1.0 - 1.0 / horizon_ref[...], (SUB, lanes))
    zero = jnp.zeros((SUB, lanes), jnp.float32)
    s, p = zero, zero + 1.0
    q1, p1, qq, qp, pp = zero, zero, zero, zero, zero
    for j in reversed(range(steps)):
        rows = pl.ds(j, SUB, stride=steps)
        factor = discount * (1.0 - dones_ref[rows, :].astype(jnp.float32))
        s = rewards_ref[rows, :] + factor * s
        p = factor * p
        q = s - center
        q1, p1 = q1 + q, p1 + p
        qq, qp, pp = qq + q * q, qp + q * p, pp + p * p
    a, b, block_sum, block_product = exclusive(s, p)
    enter_ref[0], enter_ref[1] = a, b
    rows = [
        block_sum,
        block_product,
        jnp.sum(q1 + a * p1, axis=0, keepdims=True),
        jnp.sum(b * p1, axis=0, keepdims=True),
        jnp.sum(qq + a * (2.0 * qp + a * pp), axis=0, keepdims=True),
        jnp.sum(b * (qp + a * pp), axis=0, keepdims=True),
        jnp.sum(b * b * pp, axis=0, keepdims=True),
        zero[0:1],
    ]
    table = jnp.concatenate(rows, axis=0)
    for k in range(copies):
        sent_ref[k] = table


def fold_kernel(copies, position_ref, tables_ref, bootstrap_ref, sent_ref, arrived_ref):
    blocks, _, lanes = tables_ref.shape
    position = position_ref[0]
    carry = bootstrap_ref[...]
    arrived = carry
    first = jnp.zeros_like(carry)
    second = jnp.zeros_like(carry)
    for k in reversed(range(blocks)):
        row = lambda i: tables_ref[k, i : i + 1, :]
        arrived = jnp.where(position == k, carry, arrived)
        first = first + (row(2) + carry * row(3))
        second = second + (row(4) + carry * (2.0 * row(5) + carry * row(6)))
        carry = row(0) + row(1) * carry
    arrived_ref[...] = arrived
    half = lanes // 2
    first = first + pltpu.roll(first, half, 1)
    second = second + pltpu.roll(second, half, 1)
    lane = lax.broadcasted_iota(jnp.int32, first.shape, 1)
    sent_ref[...] = jnp.broadcast_to(jnp.where(lane < half, first, second), (copies, lanes))


def scale_kernel(
    entries, mean_ref, var_ref, totals_ref, arrived_ref, enter_ref, horizon_ref, rewards_ref, dones_ref,
    out_rewards_ref, out_returns_ref, stats_ref,
):
    steps, lanes = rewards_ref.shape[0] // SUB, rewards_ref.shape[1]
    prior_mean, prior_var = mean_ref[0], var_ref[0]
    total = jnp.sum(totals_ref[...], axis=0, keepdims=True)
    lane = lax.broadcasted_iota(jnp.int32, total.shape, 1)
    first_sum = jnp.sum(jnp.where(lane < lanes // 2, total, 0.0), axis=1, keepdims=True)
    second_sum = jnp.sum(jnp.where(lane < lanes // 2, 0.0, total), axis=1, keepdims=True)
    count = jnp.float32(entries)
    merged = count + count
    delta = first_sum / count
    spread = second_sum - first_sum * delta
    new_mean = prior_mean + delta * count / merged
    new_spread = prior_var * count + spread + delta * delta * count * count / merged
    variance = new_spread / merged
    inverse = 1.0 / jnp.sqrt(variance + 1e-08)
    stats_ref[0] = new_mean[0, 0]
    stats_ref[1] = variance[0, 0]
    scale = jnp.broadcast_to(inverse, (SUB, lanes))
    discount = jnp.broadcast_to(1.0 - 1.0 / horizon_ref[...], (SUB, lanes))
    returns = enter_ref[0] + enter_ref[1] * arrived_ref[...]
    for j in reversed(range(steps)):
        rows = pl.ds(j, SUB, stride=steps)
        reward = rewards_ref[rows, :]
        factor = discount * (1.0 - dones_ref[rows, :].astype(jnp.float32))
        returns = reward + factor * returns
        out_returns_ref[rows, :] = returns * scale
        out_rewards_ref[rows, :] = reward * scale


def local(tm, env, rewards, dones, horizon, bootstrap, prior_mean, prior_var):
    steps, lanes = rewards.shape
    blocks, columns = lax.axis_size(tm), lax.axis_size(env)
    entries = steps * lanes * blocks * columns
    vmem = pl.BlockSpec(memory_space=VMEM)
    smem = pl.BlockSpec(memory_space=SMEM)
    f32 = jnp.float32
    rewards, dones = in_vmem(rewards), in_vmem(dones)
    horizon = horizon[None, :]
    sent, enter = pl.pallas_call(
        functools.partial(block_kernel, blocks),
        out_shape=(VMEM((blocks, SUB, lanes), f32), VMEM((2, SUB, lanes), f32)),
        in_specs=[smem, vmem, vmem, vmem],
        out_specs=(vmem, vmem),
        name="block_maps",
    )(prior_mean, rewards, dones, horizon)
    tables = lax.all_to_all(sent, tm, 0, 0, tiled=True)
    position = lax.axis_index(tm).astype(jnp.int32)[None]
    sent, arrived = pl.pallas_call(
        functools.partial(fold_kernel, columns),
        out_shape=(VMEM((columns, lanes), f32), VMEM((1, lanes), f32)),
        in_specs=[smem, vmem, vmem],
        out_specs=(vmem, vmem),
        name="fold_blocks",
    )(position, in_vmem(tables), bootstrap[None, :])
    totals = lax.all_to_all(sent.reshape(columns, 1, lanes), env, 0, 0, tiled=True)
    return tuple(
        pl.pallas_call(
            functools.partial(scale_kernel, entries),
            out_shape=(
                jax.ShapeDtypeStruct(rewards.shape, f32),
                jax.ShapeDtypeStruct(rewards.shape, f32),
                jax.ShapeDtypeStruct((2,), f32),
            ),
            in_specs=[smem, smem, vmem, vmem, vmem, vmem, vmem, vmem],
            out_specs=(vmem, vmem, smem),
            name="scale",
        )(
            prior_mean, prior_var, in_vmem(totals.reshape(columns, lanes)), in_vmem(arrived), in_vmem(enter),
            horizon, rewards, dones,
        )
    )


def solution(mesh):
    tm, env = mesh.axis_names
    placed = (P(tm, env), P(tm, env), P(env), P(env), P(), P())
    return jax.shard_map(
        functools.partial(local, tm, env),
        mesh=mesh,
        in_specs=placed,
        out_specs=(P(tm, env), P(tm, env), P()),
        check_vma=False,
    )
```

```python
import functools

import jax
import jax.numpy as jnp
from jax import lax
from jax.experimental import pallas as pl
from jax.experimental.pallas import tpu as pltpu
from jax.sharding import PartitionSpec as P

SUB = 8
VMEM = pltpu.VMEM
SMEM = pltpu.SMEM


def in_vmem(array):
    return pltpu.with_memory_space_constraint(array, VMEM)


def exclusive(summed, product):
    row = lax.broadcasted_iota(jnp.int32, summed.shape, 0)
    for shift in (1, 2, 4):
        inside = row < SUB - shift
        later_sum = jnp.where(inside, pltpu.roll(summed, SUB - shift, 0), 0.0)
        later_product = jnp.where(inside, pltpu.roll(product, SUB - shift, 0), 1.0)
        summed = summed + product * later_sum
        product = product * later_product
    inside = row < SUB - 1
    enter_sum = jnp.where(inside, pltpu.roll(summed, SUB - 1, 0), 0.0)
    enter_product = jnp.where(inside, pltpu.roll(product, SUB - 1, 0), 1.0)
    return enter_sum, enter_product, summed[0:1], product[0:1]


def block_kernel(
    rewards_hbm, dones_hbm, horizon_hbm, bootstrap_hbm,
    sent_ref, rewards_ref, summed_ref, product_ref, kept_ref,
    dones_ref, horizon_ref, bootstrap_ref, sems,
):
    pairs = (
        (horizon_hbm, horizon_ref), (dones_hbm, dones_ref), (rewards_hbm, rewards_ref),
        (bootstrap_hbm, bootstrap_ref),
    )
    loads = [pltpu.make_async_copy(a, b, sems.at[i]) for i, (a, b) in enumerate(pairs)]
    for load in loads:
        load.start()
    steps, _, lanes = summed_ref.shape
    zero = jnp.zeros((SUB, lanes), jnp.float32)
    s, p = zero, zero + 1.0
    s1, p1, ss, sp, pp = zero, zero, zero, zero, zero
    for load in loads:
        load.wait()
    discount = jnp.broadcast_to(1.0 - 1.0 / horizon_ref[...], (SUB, lanes))
    for j in reversed(range(steps)):
        rows = pl.ds(j, SUB, stride=steps)
        factor = discount * (1.0 - dones_ref[rows, :].astype(jnp.float32))
        s = rewards_ref[rows, :] + factor * s
        p = factor * p
        summed_ref[j], product_ref[j] = s, p
        s1, p1 = s1 + s, p1 + p
        ss, sp, pp = ss + s * s, sp + s * p, pp + p * p
    a, b, block_sum, block_product = exclusive(s, p)
    rows = [
        block_sum,
        block_product,
        jnp.sum(s1 + a * p1, axis=0, keepdims=True),
        jnp.sum(b * p1, axis=0, keepdims=True),
        jnp.sum(ss + a * (2.0 * sp + a * pp), axis=0, keepdims=True),
        jnp.sum(b * (sp + a * pp), axis=0, keepdims=True),
        jnp.sum(b * b * pp, axis=0, keepdims=True),
        zero[0:1],
    ]
    table = jnp.concatenate(rows, axis=0)
    for k in range(sent_ref.shape[0]):
        sent_ref[k] = table
    kept_ref[0], kept_ref[1] = a, b
    kept_ref[2] = jnp.broadcast_to(bootstrap_ref[...], (SUB, lanes))


def fold_kernel(tm, tables_ref, kept_ref, sent_ref, carry_ref):
    blocks, _, lanes = tables_ref.shape
    position = lax.axis_index(tm)
    carry = kept_ref[2, 0:1, :]
    arrived = carry
    first = jnp.zeros_like(carry)
    second = jnp.zeros_like(carry)
    for k in reversed(range(blocks)):
        row = lambda i: tables_ref[k, i : i + 1, :]
        arrived = jnp.where(position == k, carry, arrived)
        first = first + (row(2) + carry * row(3))
        second = second + (row(4) + carry * (2.0 * row(5) + carry * row(6)))
        carry = row(0) + row(1) * carry
    half = lanes // 2
    first = first + pltpu.roll(first, half, 1)
    second = second + pltpu.roll(second, half, 1)
    lane = lax.broadcasted_iota(jnp.int32, first.shape, 1)
    sent_ref[...] = jnp.broadcast_to(jnp.where(lane < half, first, second), sent_ref.shape)
    carry_ref[...] = kept_ref[0] + kept_ref[1] * arrived


def scale_kernel(
    entries, mean_ref, var_ref, totals_ref, carry_ref, rewards_ref, summed_ref, product_ref,
    out_rewards_hbm, out_returns_hbm, stats_hbm, scaled_rewards, scaled_returns, stats, sems,
):
    steps, _, lanes = summed_ref.shape
    prior_mean, prior_var = mean_ref[0:1, 0:1], var_ref[0:1, 0:1]
    total = jnp.sum(totals_ref[...], axis=0, keepdims=True)
    lane = lax.broadcasted_iota(jnp.int32, total.shape, 1)
    first_sum = jnp.sum(jnp.where(lane < lanes // 2, total, 0.0), axis=1, keepdims=True)
    second_sum = jnp.sum(jnp.where(lane < lanes // 2, 0.0, total), axis=1, keepdims=True)
    count = jnp.float32(entries)
    merged = count + count
    average = first_sum / count
    spread = second_sum - first_sum * average
    delta = average - prior_mean
    new_mean = prior_mean + delta * count / merged
    new_spread = prior_var * count + spread + delta * delta * count * count / merged
    variance = new_spread / merged
    inverse = 1.0 / jnp.sqrt(variance + 1e-08)
    scale = jnp.broadcast_to(inverse, (SUB, lanes))
    stores = [
        pltpu.make_async_copy(a, b, sems.at[i])
        for i, (a, b) in enumerate(
            ((scaled_returns, out_returns_hbm), (scaled_rewards, out_rewards_hbm), (stats, stats_hbm))
        )
    ]
    carry = carry_ref[...] * scale
    for j in range(steps):
        scaled_returns[pl.ds(j, SUB, stride=steps), :] = summed_ref[j] * scale + product_ref[j] * carry
    stores[0].start()
    for j in range(steps):
        rows = pl.ds(j * SUB, SUB)
        scaled_rewards[rows, :] = rewards_ref[rows, :] * scale
    stores[1].start()
    stats[0] = new_mean[0, 0]
    stats[1] = variance[0, 0]
    stores[2].start()
    for store in stores:
        store.wait()


def local(tm, env, rewards, dones, horizon, bootstrap, prior_mean, prior_var):
    rows, lanes = rewards.shape
    steps = rows // SUB
    blocks, columns = lax.axis_size(tm), lax.axis_size(env)
    entries = rows * lanes * blocks * columns
    vmem = pl.BlockSpec(memory_space=VMEM)
    hbm = pl.BlockSpec(memory_space=pltpu.HBM)
    f32 = jnp.float32
    sent, rewards_here, summed, product, kept = pl.pallas_call(
        block_kernel,
        out_shape=(
            VMEM((blocks, SUB, lanes), f32),
            VMEM((rows, lanes), f32),
            VMEM((steps, SUB, lanes), f32),
            VMEM((steps, SUB, lanes), f32),
            VMEM((3, SUB, lanes), f32),
        ),
        in_specs=[hbm] * 4,
        out_specs=(vmem,) * 5,
        scratch_shapes=[
            VMEM((rows, lanes), jnp.int32),
            VMEM((1, lanes), f32),
            VMEM((1, lanes), f32),
            pltpu.SemaphoreType.DMA((4,)),
        ],
        name="block_maps",
    )(rewards, dones, horizon[None, :], bootstrap[None, :])
    tables = lax.all_to_all(sent, tm, 0, 0, tiled=True)
    sent, carry = pl.pallas_call(
        functools.partial(fold_kernel, tm),
        out_shape=(VMEM((columns, lanes), f32), VMEM((SUB, lanes), f32)),
        in_specs=[vmem, vmem],
        out_specs=(vmem, vmem),
        name="fold_blocks",
    )(in_vmem(tables), in_vmem(kept))
    totals = lax.all_to_all(sent.reshape(columns, 1, lanes), env, 0, 0, tiled=True)
    totals = totals.reshape(columns, lanes)
    return tuple(
        pl.pallas_call(
            functools.partial(scale_kernel, entries),
            out_shape=(
                jax.ShapeDtypeStruct((rows, lanes), f32),
                jax.ShapeDtypeStruct((rows, lanes), f32),
                jax.ShapeDtypeStruct((2,), f32),
            ),
            in_specs=[vmem] * 7,
            out_specs=(hbm,) * 3,
            scratch_shapes=[
                VMEM((rows, lanes), f32),
                VMEM((rows, lanes), f32),
                SMEM((2,), f32),
                pltpu.SemaphoreType.DMA((3,)),
            ],
            name="scale",
        )(prior_mean[None], prior_var[None], *map(in_vmem, (totals, carry, rewards_here, summed, product)))
    )


def solution(mesh):
    tm, env = mesh.axis_names
    placed = (P(tm, env), P(tm, env), P(env), P(env), P(), P())
    return jax.shard_map(
        functools.partial(local, tm, env),
        mesh=mesh,
        in_specs=placed,
        out_specs=(P(tm, env), P(tm, env), P()),
        check_vma=False,
    )
```

```python
import functools

import jax
import jax.numpy as jnp
from jax import lax
from jax.experimental import pallas as pl
from jax.experimental.pallas import tpu as pltpu
from jax.sharding import PartitionSpec as P

SUB = 8
VMEM = pltpu.VMEM
SMEM = pltpu.SMEM


def in_vmem(array):
    return pltpu.with_memory_space_constraint(array, VMEM)


def exclusive(summed, product):
    row = lax.broadcasted_iota(jnp.int32, summed.shape, 0)
    for shift in (1, 2, 4):
        inside = row < SUB - shift
        later_sum = jnp.where(inside, pltpu.roll(summed, SUB - shift, 0), 0.0)
        later_product = jnp.where(inside, pltpu.roll(product, SUB - shift, 0), 1.0)
        summed = summed + product * later_sum
        product = product * later_product
    inside = row < SUB - 1
    enter_sum = jnp.where(inside, pltpu.roll(summed, SUB - 1, 0), 0.0)
    enter_product = jnp.where(inside, pltpu.roll(product, SUB - 1, 0), 1.0)
    return enter_sum, enter_product, summed[0:1], product[0:1]


def block_kernel(
    prior_ref, rewards_hbm, dones_hbm, horizon_hbm, bootstrap_hbm,
    sent_ref, rewards_ref, summed_ref, product_ref, kept_ref,
    dones_ref, horizon_ref, bootstrap_ref, sems,
):
    pairs = (
        (horizon_hbm, horizon_ref), (dones_hbm, dones_ref), (rewards_hbm, rewards_ref),
        (bootstrap_hbm, bootstrap_ref),
    )
    loads = [pltpu.make_async_copy(a, b, sems.at[i]) for i, (a, b) in enumerate(pairs)]
    for load in loads:
        load.start()
    steps, _, lanes = summed_ref.shape
    zero = jnp.zeros((SUB, lanes), jnp.float32)
    s, p = zero, zero + 1.0
    s1, p1, ss, sp, pp = zero, zero, zero, zero, zero
    for load in loads:
        load.wait()
    discount = jnp.broadcast_to(1.0 - 1.0 / horizon_ref[...], (SUB, lanes))
    for j in reversed(range(steps)):
        rows = pl.ds(j, SUB, stride=steps)
        factor = discount * (1.0 - dones_ref[rows, :].astype(jnp.float32))
        s = rewards_ref[rows, :] + factor * s
        p = factor * p
        summed_ref[j], product_ref[j] = s, p
        s1, p1 = s1 + s, p1 + p
        ss, sp, pp = ss + s * s, sp + s * p, pp + p * p
    a, b, block_sum, block_product = exclusive(s, p)
    rows = [
        block_sum,
        block_product,
        jnp.sum(s1 + a * p1, axis=0, keepdims=True),
        jnp.sum(b * p1, axis=0, keepdims=True),
        jnp.sum(ss + a * (2.0 * sp + a * pp), axis=0, keepdims=True),
        jnp.sum(b * (sp + a * pp), axis=0, keepdims=True),
        jnp.sum(b * b * pp, axis=0, keepdims=True),
        prior_ref[...],
    ]
    table = jnp.concatenate(rows, axis=0)
    for k in range(sent_ref.shape[0]):
        sent_ref[k] = table
    kept_ref[0], kept_ref[1] = a, b
    kept_ref[2] = jnp.broadcast_to(bootstrap_ref[...], (SUB, lanes))


def fold_kernel(tm, tables_ref, kept_ref, sent_ref, carry_ref):
    blocks, _, lanes = tables_ref.shape
    position = lax.axis_index(tm)
    carry = kept_ref[2, 0:1, :]
    arrived = carry
    first = jnp.zeros_like(carry)
    second = jnp.zeros_like(carry)
    for k in reversed(range(blocks)):
        row = lambda i: tables_ref[k, i : i + 1, :]
        arrived = jnp.where(position == k, carry, arrived)
        first = first + (row(2) + carry * row(3))
        second = second + (row(4) + carry * (2.0 * row(5) + carry * row(6)))
        carry = row(0) + row(1) * carry
    half = lanes // 2
    first = first + pltpu.roll(first, half, 1)
    second = second + pltpu.roll(second, half, 1)
    lane = lax.broadcasted_iota(jnp.int32, first.shape, 1)
    sent_ref[...] = jnp.broadcast_to(jnp.where(lane < half, first, second), sent_ref.shape)
    carry_ref[0] = kept_ref[0] + kept_ref[1] * arrived
    carry_ref[1] = jnp.broadcast_to(tables_ref[0, SUB - 1 : SUB, :], (SUB, lanes))
    carry_ref[2] = jnp.broadcast_to(tables_ref[1, SUB - 1 : SUB, :], (SUB, lanes))


def scale_kernel(
    entries, totals_ref, carry_ref, rewards_ref, summed_ref, product_ref,
    out_rewards_hbm, out_returns_hbm, stats_hbm, scaled_rewards, scaled_returns, stats, sems,
):
    steps, _, lanes = summed_ref.shape
    prior_mean, prior_var = carry_ref[1, 0:1, 0:1], carry_ref[2, 0:1, 0:1]
    total = jnp.sum(totals_ref[...], axis=0, keepdims=True)
    lane = lax.broadcasted_iota(jnp.int32, total.shape, 1)
    first_sum = jnp.sum(jnp.where(lane < lanes // 2, total, 0.0), axis=1, keepdims=True)
    second_sum = jnp.sum(jnp.where(lane < lanes // 2, 0.0, total), axis=1, keepdims=True)
    count = jnp.float32(entries)
    merged = count + count
    average = first_sum / count
    spread = second_sum - first_sum * average
    delta = average - prior_mean
    new_mean = prior_mean + delta * count / merged
    new_spread = prior_var * count + spread + delta * delta * count * count / merged
    variance = new_spread / merged
    inverse = 1.0 / jnp.sqrt(variance + 1e-08)
    scale = jnp.broadcast_to(inverse, (SUB, lanes))
    stores = [
        pltpu.make_async_copy(a, b, sems.at[i])
        for i, (a, b) in enumerate(
            ((scaled_returns, out_returns_hbm), (scaled_rewards, out_rewards_hbm), (stats, stats_hbm))
        )
    ]
    carry = carry_ref[0] * scale
    for j in range(steps):
        scaled_returns[pl.ds(j, SUB, stride=steps), :] = summed_ref[j] * scale + product_ref[j] * carry
    stores[0].start()
    for j in range(steps):
        rows = pl.ds(j * SUB, SUB)
        scaled_rewards[rows, :] = rewards_ref[rows, :] * scale
    stores[1].start()
    stats[0] = new_mean[0, 0]
    stats[1] = variance[0, 0]
    stores[2].start()
    for store in stores:
        store.wait()


def local(tm, env, rewards, dones, horizon, bootstrap, prior_mean, prior_var):
    rows, lanes = rewards.shape
    steps = rows // SUB
    blocks, columns = lax.axis_size(tm), lax.axis_size(env)
    entries = rows * lanes * blocks * columns
    vmem = pl.BlockSpec(memory_space=VMEM)
    hbm = pl.BlockSpec(memory_space=pltpu.HBM)
    f32 = jnp.float32
    row = lambda scalar: lambda _: jnp.broadcast_to(scalar, (1, lanes))
    prior = lax.switch(
        jnp.minimum(lax.axis_index(tm), 2),
        (row(prior_mean), row(prior_var), lambda _: jnp.zeros((1, lanes), f32)),
        0,
    )
    sent, rewards_here, summed, product, kept = pl.pallas_call(
        block_kernel,
        out_shape=(
            VMEM((blocks, SUB, lanes), f32),
            VMEM((rows, lanes), f32),
            VMEM((steps, SUB, lanes), f32),
            VMEM((steps, SUB, lanes), f32),
            VMEM((3, SUB, lanes), f32),
        ),
        in_specs=[vmem] + [hbm] * 4,
        out_specs=(vmem,) * 5,
        scratch_shapes=[
            VMEM((rows, lanes), jnp.int32),
            VMEM((1, lanes), f32),
            VMEM((1, lanes), f32),
            pltpu.SemaphoreType.DMA((4,)),
        ],
        name="block_maps",
    )(in_vmem(prior), rewards, dones, horizon[None, :], bootstrap[None, :])
    tables = lax.all_to_all(sent, tm, 0, 0, tiled=True)
    sent, carry = pl.pallas_call(
        functools.partial(fold_kernel, tm),
        out_shape=(VMEM((columns, lanes), f32), VMEM((3, SUB, lanes), f32)),
        in_specs=[vmem, vmem],
        out_specs=(vmem, vmem),
        name="fold_blocks",
    )(in_vmem(tables), in_vmem(kept))
    totals = lax.all_to_all(sent.reshape(columns, 1, lanes), env, 0, 0, tiled=True)
    totals = totals.reshape(columns, lanes)
    return tuple(
        pl.pallas_call(
            functools.partial(scale_kernel, entries),
            out_shape=(
                jax.ShapeDtypeStruct((rows, lanes), f32),
                jax.ShapeDtypeStruct((rows, lanes), f32),
                jax.ShapeDtypeStruct((2,), f32),
            ),
            in_specs=[vmem] * 5,
            out_specs=(hbm,) * 3,
            scratch_shapes=[
                VMEM((rows, lanes), f32),
                VMEM((rows, lanes), f32),
                SMEM((2,), f32),
                pltpu.SemaphoreType.DMA((3,)),
            ],
            name="scale",
        )(*map(in_vmem, (totals, carry, rewards_here, summed, product)))
    )


def solution(mesh):
    tm, env = mesh.axis_names
    placed = (P(tm, env), P(tm, env), P(env), P(env), P(), P())
    return jax.shard_map(
        functools.partial(local, tm, env),
        mesh=mesh,
        in_specs=placed,
        out_specs=(P(tm, env), P(tm, env), P()),
        check_vma=False,
    )
```

```python
import functools

import jax
import jax.numpy as jnp
from jax import lax
from jax.experimental import pallas as pl
from jax.experimental.pallas import tpu as pltpu
from jax.sharding import PartitionSpec as P

SUB = 8
TM_FIRST, ENV_FIRST = 11, 20
VMEM = pltpu.VMEM
SMEM = pltpu.SMEM


def in_vmem(array):
    return pltpu.with_memory_space_constraint(array, VMEM)


def headed(count, first):
    first = first % count
    return [first] + [i for i in range(count) if i != first]


def exclusive(summed, product):
    row = lax.broadcasted_iota(jnp.int32, summed.shape, 0)
    for shift in (1, 2, 4):
        inside = row < SUB - shift
        later_sum = jnp.where(inside, pltpu.roll(summed, SUB - shift, 0), 0.0)
        later_product = jnp.where(inside, pltpu.roll(product, SUB - shift, 0), 1.0)
        summed = summed + product * later_sum
        product = product * later_product
    inside = row < SUB - 1
    enter_sum = jnp.where(inside, pltpu.roll(summed, SUB - 1, 0), 0.0)
    enter_product = jnp.where(inside, pltpu.roll(product, SUB - 1, 0), 1.0)
    return enter_sum, enter_product, summed[0:1], product[0:1]


def block_kernel(
    prior_ref, rewards_hbm, dones_hbm, horizon_hbm, bootstrap_hbm,
    sent_ref, rewards_ref, summed_ref, product_ref, kept_ref,
    dones_ref, horizon_ref, bootstrap_ref, sems,
):
    pairs = (
        (horizon_hbm, horizon_ref), (dones_hbm, dones_ref), (rewards_hbm, rewards_ref),
        (bootstrap_hbm, bootstrap_ref),
    )
    loads = [pltpu.make_async_copy(a, b, sems.at[i]) for i, (a, b) in enumerate(pairs)]
    for load in loads:
        load.start()
    steps, _, lanes = summed_ref.shape
    zero = jnp.zeros((SUB, lanes), jnp.float32)
    s, p = zero, zero + 1.0
    s1, p1, ss, sp, pp = zero, zero, zero, zero, zero
    for load in loads:
        load.wait()
    discount = jnp.broadcast_to(1.0 - 1.0 / horizon_ref[...], (SUB, lanes))
    for j in reversed(range(steps)):
        rows = pl.ds(j, SUB, stride=steps)
        factor = discount * (1.0 - dones_ref[rows, :].astype(jnp.float32))
        s = rewards_ref[rows, :] + factor * s
        p = factor * p
        summed_ref[j], product_ref[j] = s, p
        s1, p1 = s1 + s, p1 + p
        ss, sp, pp = ss + s * s, sp + s * p, pp + p * p
    a, b, block_sum, block_product = exclusive(s, p)
    rows = [
        block_sum,
        block_product,
        jnp.sum(s1 + a * p1, axis=0, keepdims=True),
        jnp.sum(b * p1, axis=0, keepdims=True),
        jnp.sum(ss + a * (2.0 * sp + a * pp), axis=0, keepdims=True),
        jnp.sum(b * (sp + a * pp), axis=0, keepdims=True),
        jnp.sum(b * b * pp, axis=0, keepdims=True),
        prior_ref[...],
    ]
    table = jnp.concatenate(rows, axis=0)
    for k in range(sent_ref.shape[0]):
        sent_ref[k] = table
    kept_ref[0], kept_ref[1] = a, b
    kept_ref[2] = jnp.broadcast_to(bootstrap_ref[...], (SUB, lanes))


def fold_kernel(tm, tables_ref, kept_ref, sent_ref, carry_ref):
    blocks, _, lanes = tables_ref.shape
    position = lax.axis_index(tm)
    order = headed(blocks, TM_FIRST)
    carry = kept_ref[2, 0:1, :]
    arrived = carry
    first = jnp.zeros_like(carry)
    second = jnp.zeros_like(carry)
    for k in reversed(range(blocks)):
        row = lambda i: tables_ref[order.index(k), i : i + 1, :]
        arrived = jnp.where(position == k, carry, arrived)
        first = first + (row(2) + carry * row(3))
        second = second + (row(4) + carry * (2.0 * row(5) + carry * row(6)))
        carry = row(0) + row(1) * carry
    half = lanes // 2
    first = first + pltpu.roll(first, half, 1)
    second = second + pltpu.roll(second, half, 1)
    lane = lax.broadcasted_iota(jnp.int32, first.shape, 1)
    sent_ref[...] = jnp.broadcast_to(jnp.where(lane < half, first, second), sent_ref.shape)
    carry_ref[0] = kept_ref[0] + kept_ref[1] * arrived
    carry_ref[1] = jnp.broadcast_to(tables_ref[order.index(0), SUB - 1 : SUB, :], (SUB, lanes))
    carry_ref[2] = jnp.broadcast_to(tables_ref[order.index(1), SUB - 1 : SUB, :], (SUB, lanes))


def scale_kernel(
    entries, totals_ref, carry_ref, rewards_ref, summed_ref, product_ref,
    out_rewards_hbm, out_returns_hbm, stats_hbm, scaled_rewards, scaled_returns, stats, sems,
):
    steps, _, lanes = summed_ref.shape
    prior_mean, prior_var = carry_ref[1, 0:1, 0:1], carry_ref[2, 0:1, 0:1]
    total = jnp.sum(totals_ref[...], axis=0, keepdims=True)
    lane = lax.broadcasted_iota(jnp.int32, total.shape, 1)
    first_sum = jnp.sum(jnp.where(lane < lanes // 2, total, 0.0), axis=1, keepdims=True)
    second_sum = jnp.sum(jnp.where(lane < lanes // 2, 0.0, total), axis=1, keepdims=True)
    count = jnp.float32(entries)
    merged = count + count
    average = first_sum / count
    spread = second_sum - first_sum * average
    delta = average - prior_mean
    new_mean = prior_mean + delta * count / merged
    new_spread = prior_var * count + spread + delta * delta * count * count / merged
    variance = new_spread / merged
    inverse = 1.0 / jnp.sqrt(variance + 1e-08)
    scale = jnp.broadcast_to(inverse, (SUB, lanes))
    stores = [
        pltpu.make_async_copy(a, b, sems.at[i])
        for i, (a, b) in enumerate(
            ((scaled_returns, out_returns_hbm), (scaled_rewards, out_rewards_hbm), (stats, stats_hbm))
        )
    ]
    carry = carry_ref[0] * scale
    for j in range(steps):
        scaled_returns[pl.ds(j, SUB, stride=steps), :] = summed_ref[j] * scale + product_ref[j] * carry
    stores[0].start()
    for j in range(steps):
        rows = pl.ds(j * SUB, SUB)
        scaled_rewards[rows, :] = rewards_ref[rows, :] * scale
    stores[1].start()
    stats[0] = new_mean[0, 0]
    stats[1] = variance[0, 0]
    stores[2].start()
    for store in stores:
        store.wait()


def local(tm, env, rewards, dones, horizon, bootstrap, prior_mean, prior_var):
    rows, lanes = rewards.shape
    steps = rows // SUB
    blocks, columns = lax.axis_size(tm), lax.axis_size(env)
    entries = rows * lanes * blocks * columns
    vmem = pl.BlockSpec(memory_space=VMEM)
    hbm = pl.BlockSpec(memory_space=pltpu.HBM)
    f32 = jnp.float32
    row = lambda scalar: lambda _: jnp.broadcast_to(scalar, (1, lanes))
    prior = lax.switch(
        jnp.minimum(lax.axis_index(tm), 2),
        (row(prior_mean), row(prior_var), lambda _: jnp.zeros((1, lanes), f32)),
        0,
    )
    sent, rewards_here, summed, product, kept = pl.pallas_call(
        block_kernel,
        out_shape=(
            VMEM((blocks, SUB, lanes), f32),
            VMEM((rows, lanes), f32),
            VMEM((steps, SUB, lanes), f32),
            VMEM((steps, SUB, lanes), f32),
            VMEM((3, SUB, lanes), f32),
        ),
        in_specs=[vmem] + [hbm] * 4,
        out_specs=(vmem,) * 5,
        scratch_shapes=[
            VMEM((rows, lanes), jnp.int32),
            VMEM((1, lanes), f32),
            VMEM((1, lanes), f32),
            pltpu.SemaphoreType.DMA((4,)),
        ],
        name="block_maps",
    )(in_vmem(prior), rewards, dones, horizon[None, :], bootstrap[None, :])
    tables = lax.all_to_all(sent, tm, 0, 0, tiled=True, axis_index_groups=[headed(blocks, TM_FIRST)])
    sent, carry = pl.pallas_call(
        functools.partial(fold_kernel, tm),
        out_shape=(VMEM((columns, lanes), f32), VMEM((3, SUB, lanes), f32)),
        in_specs=[vmem, vmem],
        out_specs=(vmem, vmem),
        name="fold_blocks",
    )(in_vmem(tables), in_vmem(kept))
    totals = lax.all_to_all(sent.reshape(columns, 1, lanes), env, 0, 0, tiled=True, axis_index_groups=[headed(columns, ENV_FIRST)])
    totals = totals.reshape(columns, lanes)
    return tuple(
        pl.pallas_call(
            functools.partial(scale_kernel, entries),
            out_shape=(
                jax.ShapeDtypeStruct((rows, lanes), f32),
                jax.ShapeDtypeStruct((rows, lanes), f32),
                jax.ShapeDtypeStruct((2,), f32),
            ),
            in_specs=[vmem] * 5,
            out_specs=(hbm,) * 3,
            scratch_shapes=[
                VMEM((rows, lanes), f32),
                VMEM((rows, lanes), f32),
                SMEM((2,), f32),
                pltpu.SemaphoreType.DMA((3,)),
            ],
            name="scale",
        )(*map(in_vmem, (totals, carry, rewards_here, summed, product)))
    )


def solution(mesh):
    tm, env = mesh.axis_names
    placed = (P(tm, env), P(tm, env), P(env), P(env), P(), P())
    return jax.shard_map(
        functools.partial(local, tm, env),
        mesh=mesh,
        in_specs=placed,
        out_specs=(P(tm, env), P(tm, env), P()),
        check_vma=False,
    )
```
